32 devices in a mesh: groups: 2 (over y), feat: 4 (over z), head: 4 (over x, core).
Axes of the slice: x: 2, y: 2, z: 4, core: 2. Of those that a mesh axis runs over, the one named last changes fastest.
Arguments:
- token_ids: int32 [32], P('groups'), parts along dimension 0, may hold values from 0 to 75967
- embedding: bfloat16 [75968, 5120], P('head', 'feat'), may hold values from -16 to 16
- retained: bfloat16 [2, 32, 8, 8256, 128], P(None, 'groups', 'head', 'feat'), parts along dimension 1, may hold values from -0.29882812 to 0.29882812
- query_weight: bfloat16 [2, 5120, 5120], P(None, 'feat', 'head'), may hold values from -0.078125 to 0.078125
- key_weight: bfloat16 [2, 5120, 1024], P(None, 'feat', 'head'), may hold values from -0.078125 to 0.078125
- value_weight: bfloat16 [2, 5120, 1024], P(None, 'feat', 'head'), may hold values from -0.078125 to 0.078125
- gate_weight: bfloat16 [2, 5120, 8], P(None, 'feat', 'head'), may hold values from -0.078125 to 0.078125
- gate_bias: float32 [2, 8], P(None, 'head'), may hold values from -4 to 3
- norm_gain: float32 [2, 5120], P(None, 'feat'), may hold values from 0.1 to 1.9
- read_gain: float32 [2, 128], replicated, may hold values from 0.1 to 1.9
- out_weight: bfloat16 [2, 5120, 5120], P(None, 'head', 'feat'), may hold values from -0.078125 to 0.078125
Outputs:
- hidden_out: bfloat16 [32, 5120], P('groups', 'feat'), parts along dimension 0
The draws below stay inside these ranges and needn't reach their ends.
There are 2 independent parts, one for each index of `groups`. The reference program is written for one: setup_inputs(seed, part) draws one part's arguments, and reference() takes and returns one part's arrays. A program takes and returns all parts, laid end to end along the dimension named above; an argument that names none is the same for every part. Nothing has to cross between parts.
All inputs are finite; a program needn't handle non-finite values.
Results may differ from the reference program's by a relative error of at most 0.01345.
The reference program's roundings to bfloat16 on the way (of `stream`, `normed` and `mixed`) count: a program that leaves them out, or rounds other values in their place, can miss the bound.
Values may be sent and summed in bfloat16 or wider, within the bound.
A program may use at most 192 MiB of HBM per device.

```python
import math
import jax
import jax.numpy as jnp
import numpy as np
from jax import lax

D = 5120
QH = 40
KVH = 8
HD = 128
VOCAB = 75968
LAYERS = 2
REQ = 16
FEAT = 8256


def draw_embedding(key, part):
    key_base = jax.random.fold_in(key, 11)
    key_rows = jax.random.fold_in(key, 12)
    column = jnp.arange(D, dtype=jnp.float32) / max(D - 1, 1)
    row_scale = jnp.exp(jax.random.uniform(key_rows, (VOCAB, 1), minval=0.0, maxval=math.log(10.0)))
    rising = jnp.exp(math.log(3.0) * column)
    noise = jax.random.normal(key_base, (VOCAB, D))
    return jnp.clip(0.05 * noise * row_scale * rising, -16.0, 16.0).astype(jnp.bfloat16)


def plant(drawn, own_key, smallest, top_value):
    extent = drawn.shape
    index_at = [jax.random.randint(jax.random.fold_in(own_key, axis), (), 0, extent[axis]) for axis in range(len(extent))]
    drawn = drawn.at[tuple(index_at)].set(smallest)
    longest = extent.index(max(extent))
    index_at[longest] = (index_at[longest] + 1) % extent[longest]
    return drawn.at[tuple(index_at)].set(top_value)


def block_levels(rng, shape, cuts, least, top_value):
    def one(axis_at, parts):
        draws = jax.random.uniform(jax.random.fold_in(jax.random.fold_in(rng, 6), axis_at), (parts,), jnp.float32, least / len(cuts), top_value / len(cuts))
        return jnp.repeat(jnp.exp(draws), shape[axis_at] // parts).reshape((-1,) + (1,) * (len(shape) - axis_at - 1))

    loudness = one(*cuts[0])
    for cut in cuts[1:]:
        loudness = loudness * one(*cut)
    return loudness


def scatter_about(own_key, dims, scale, reach, shards=(), kind=jnp.bfloat16):
    factor_of = block_levels(own_key, dims, shards, -0.22, 0.18) if shards else 1.0
    values = jax.random.normal(own_key, dims, jnp.float32) * scale * factor_of
    return jnp.minimum(jnp.maximum(values, -reach), reach).astype(kind)


def setup_inputs(seed: int = 0, part: int = 0) -> dict:
    key_list = jax.random.split(jax.random.key(seed), 12)
    part_keys = jax.random.split(jax.random.fold_in(key_list[11], part), 12)
    return {
        "token_ids": plant(jax.random.randint(part_keys[0], (REQ,), 0, VOCAB), jax.random.fold_in(part_keys[0], 1), 0, VOCAB - 1).astype(jnp.int32),
        "embedding": draw_embedding(jax.random.fold_in(key_list[11], 71), part),
        "retained": scatter_about(part_keys[2], (LAYERS, REQ, KVH, FEAT, HD), 0.05, 0.29882812, ((2, 4), (3, 4))),
        "query_weight": scatter_about(key_list[3], (LAYERS, D, QH * HD), D ** -0.5, 0.078125, ((1, 4), (2, 4))),
        "key_weight": scatter_about(key_list[4], (LAYERS, D, KVH * HD), D ** -0.5, 0.078125, ((1, 4), (2, 4))),
        "value_weight": scatter_about(key_list[5], (LAYERS, D, KVH * HD), D ** -0.5, 0.078125, ((1, 4), (2, 4))),
        "gate_weight": scatter_about(key_list[6], (LAYERS, D, KVH), D ** -0.5, 0.078125, ((1, 4), (2, 4))),
        "gate_bias": jnp.clip(-4.0 + 7.0 * jax.random.uniform(key_list[7], (LAYERS, KVH), jnp.float32) ** block_levels(key_list[7], (LAYERS, KVH), ((1, 4),), -0.2, 0.2), -4.0, 3.0),
        "norm_gain": jnp.clip(1.0 + 0.18 * jax.random.normal(key_list[8], (LAYERS, D), jnp.float32), 0.1, 1.9),
        "read_gain": jnp.clip(1.0 + 0.18 * jax.random.normal(key_list[9], (LAYERS, HD), jnp.float32), 0.1, 1.9),
        "out_weight": scatter_about(key_list[10], (LAYERS, QH * HD, D), (QH * HD) ** -0.5, 0.078125, ((1, 4), (2, 4))),
    }


def reference(token_ids, embedding, retained, query_weight, key_weight, value_weight, gate_weight, gate_bias, norm_gain, read_gain, out_weight):
    pair_left, pair_right = np.triu_indices(HD)
    pair_left = jnp.asarray(pair_left.astype(np.int32))
    pair_right = jnp.asarray(pair_right.astype(np.int32))
    pair_scale = jnp.where(pair_left == pair_right, 1.0, math.sqrt(2.0)).astype(jnp.float32)
    stream = jnp.take(embedding, token_ids, axis=0)
    for layer_index in range(LAYERS):
        stream_wide = stream.astype(jnp.float32)
        sum_sq = lax.optimization_barrier(jnp.sum(stream_wide * stream_wide, axis=-1, keepdims=True))
        normed = (stream_wide * lax.rsqrt(sum_sq / D + 1e-06) * norm_gain[layer_index]).astype(jnp.bfloat16)
        query = jnp.dot(normed, query_weight[layer_index], preferred_element_type=jnp.float32).astype(jnp.bfloat16)
        query = query.reshape(REQ, KVH, QH // KVH, HD)
        key_rows = jnp.dot(normed, key_weight[layer_index], preferred_element_type=jnp.float32).astype(jnp.bfloat16)
        key_rows = key_rows.reshape(REQ, KVH, HD)
        value_rows = jnp.dot(normed, value_weight[layer_index], preferred_element_type=jnp.float32).astype(jnp.bfloat16)
        value_rows = value_rows.reshape(REQ, KVH, HD)
        gate_logit = jnp.dot(normed, gate_weight[layer_index], preferred_element_type=jnp.float32)
        decay_rate = jnp.exp(-jax.nn.softplus(gate_logit + gate_bias[layer_index]))
        query_wide = query.astype(jnp.float32)
        phi_query = (query_wide[..., pair_left] * query_wide[..., pair_right] * pair_scale).astype(jnp.bfloat16)
        key_wide = key_rows.astype(jnp.float32)
        phi_key = (key_wide[..., pair_left] * key_wide[..., pair_right] * pair_scale / HD).astype(jnp.bfloat16)
        history = jnp.einsum('rhgf,rhfe->rhge', phi_query.astype(jnp.float32), retained[layer_index].astype(jnp.float32))
        cross_term = jnp.einsum('rhgf,rhf->rhg', phi_query.astype(jnp.float32), phi_key.astype(jnp.float32))
        readout = decay_rate[:, :, None, None] * history + cross_term[..., None] * value_rows.astype(jnp.float32)[:, :, None, :]
        scaled = readout * lax.rsqrt(lax.optimization_barrier(jnp.mean(readout * readout, axis=-1, keepdims=True)) + 1e-06) * read_gain[layer_index]
        mixed = scaled.astype(jnp.bfloat16).reshape(REQ, QH * HD)
        branch = jnp.dot(mixed, out_weight[layer_index], preferred_element_type=jnp.float32)
        stream = (stream_wide + branch).astype(jnp.bfloat16)
    return stream
```

```python
import functools
import math

import jax
import jax.numpy as jnp
from jax import lax
from jax.experimental import pallas as pl
from jax.experimental.pallas import tpu as pltpu
from jax.sharding import PartitionSpec as P

MESH = pl.DeviceIdType.MESH
F32 = jnp.float32
BF16 = jnp.bfloat16
LANES = 128


def lookup(ids_ref, table_hbm, picked_ref, rows_buf, row_sem):
    requests, width = picked_ref.shape
    table_rows = table_hbm.shape[0]
    base = lax.axis_index("head") * table_rows
    window = rows_buf.shape[0] // requests
    out_row = lax.broadcasted_iota(jnp.int32, (requests, requests * window), 0)
    column = lax.broadcasted_iota(jnp.int32, (requests, requests * window), 1)
    select = jnp.zeros((requests, requests * window), F32)
    copies = []
    for i in range(requests):
        local = ids_ref[i] - base
        row = jnp.clip(local, 0, table_rows - 1)
        first = pl.multiple_of(jnp.minimum((row // 8) * 8, table_rows - window), 8)
        copy = pltpu.make_async_copy(
            table_hbm.at[pl.ds(first, window)],
            rows_buf.at[pl.ds(i * window, window)],
            row_sem.at[i],
        )
        copy.start()
        copies.append(copy)
        value = jnp.where(local == row, 1.0, 0.0)
        hit = (out_row == i) & (column == i * window + row - first)
        select = jnp.where(hit, value, select)
    for copy in copies:
        copy.wait()
    picked_ref[...] = jnp.dot(
        select.astype(BF16), rows_buf[...], preferred_element_type=F32
    ).astype(BF16)


def partner_of(me, count, turn):
    if count == 4:
        return (3 - me, lax.rem(me + 2, 4), me + 1 - 2 * lax.rem(me, 2))[turn - 1]
    return lax.rem(me + turn, count)


def kernel(
    feat_count,
    head_count,
    parts,
    picked_ref,
    retained_hbm,
    query_hbm,
    key_hbm,
    value_hbm,
    gate_hbm,
    bias_hbm,
    gain_hbm,
    read_hbm,
    out_hbm,
    result_ref,
    state,
    query_w,
    key_w,
    value_w,
    gate_w,
    bias_ref,
    gain_ref,
    read_ref,
    out_w,
    pick_buf,
    lead_buf,
    query_buf,
    pair_buf,
    read_buf,
    branch_buf,
    left_sel,
    right_sel,
    pair_scale,
    phi,
    history,
    load_sem,
    state_sem,
    send_sem,
    recv_sem,
):
    layers, requests, heads, block, head_size = state.shape
    width = query_w.shape[1]
    query_columns = query_w.shape[2]
    kv_columns = key_w.shape[2]
    chunks, chunk = branch_buf.shape[2], branch_buf.shape[5]
    group = query_columns // (heads * head_size)
    span = group * head_size
    n = requests // parts
    me_feat = lax.axis_index("feat")
    me_head = lax.axis_index("head")

    barrier = pltpu.get_barrier_semaphore()
    for axis, count, me in (("feat", feat_count, me_feat), ("head", head_count, me_head)):
        for d in range(1, count):
            pl.semaphore_signal(
                barrier, inc=1, device_id={axis: lax.rem(me + d, count)}, device_id_type=MESH
            )

    load = {}

    def start_load(slot, source, target, layer):
        load[layer, slot] = pltpu.make_async_copy(source, target, load_sem.at[layer, slot])
        load[layer, slot].start()

    def load_inputs(layer):
        pairs = [(gate_hbm, gate_w), (query_hbm, query_w), (key_hbm, key_w), (value_hbm, value_w)]
        for slot, (source, target) in enumerate(pairs):
            start_load(slot, source.at[layer], target.at[layer], layer)

    def load_state(layer):
        for r in range(requests):
            pltpu.make_async_copy(
                retained_hbm.at[layer, r], state.at[layer, r], state_sem.at[layer, r]
            ).start()
        start_load(4, out_hbm.at[layer], out_w.at[layer], layer)

    start_load(5, gain_hbm, gain_ref, 0)
    start_load(6, bias_hbm, bias_ref, 0)
    start_load(7, read_hbm, read_ref, 0)
    load_inputs(0)
    pl.semaphore_wait(barrier, feat_count + head_count - 2)

    sent = []

    def exchange(axis, count, me, source, target):
        copies = []
        for d in range(1, count):
            copy = pltpu.make_async_remote_copy(
                src_ref=source,
                dst_ref=target,
                send_sem=send_sem.at[len(sent)],
                recv_sem=recv_sem.at[len(sent)],
                device_id={axis: partner_of(me, count, d)},
                device_id_type=MESH,
            )
            copy.start()
            copies.append(copy)
            sent.append(copy)
        return copies

    def arrive(copies):
        for copy in copies:
            copy.wait_recv()

    pick_copies = []
    for p in range(parts):
        rows = slice(p * n, (p + 1) * n)
        pick_copies.append(
            exchange(
                "head", head_count, me_head, picked_ref.at[rows], pick_buf.at[p, me_head]
            )
        )
    load_state(0)
    for layer in range(1, layers):
        load_inputs(layer)
        load_state(layer)

    feature = lax.broadcasted_iota(jnp.int32, (head_size, block), 1) + me_feat * block
    position = lax.broadcasted_iota(jnp.int32, (head_size, block), 0)
    begin = position * head_size - (position * (position - 1)) // 2
    inside = (feature >= begin) & (feature < begin + head_size - position)
    left_sel[...] = jnp.where(inside, 1.0, 0.0).astype(BF16)
    partner = jnp.sum(jnp.where(inside, feature - begin + position, 0), axis=0, keepdims=True)
    right_sel[...] = jnp.where(position == partner, 1.0, 0.0).astype(BF16)
    first = jnp.sum(jnp.where(inside, position, 0), axis=0, keepdims=True)
    pair_scale[...] = jnp.where(first == partner, 1.0, math.sqrt(2.0)).astype(F32)
    phi[...] = jnp.zeros(phi.shape, F32)

    for slot in (5, 6, 7):
        load[0, slot].wait()

    fields = heads + 1
    lane = lax.broadcasted_iota(jnp.int32, (n, LANES), 1)
    unroll = 4 if n % 4 == 0 else 1
    stream = [None] * parts
    branch_copies = [None] * parts

    for p in range(parts):
        pick_buf[p, me_head] = picked_ref[p * n : (p + 1) * n, :]

    for layer in range(layers):
        lead_copies, query_copies, pair_copies = [], [], []
        for p in range(parts):
            if layer == 0:
                arrive(pick_copies[p])
                total = pick_buf[p, 0].astype(F32)
                for i in range(1, head_count):
                    total = total + pick_buf[p, i].astype(F32)
                stream[p] = total
            else:
                stream[p] = finish(p, layer - 1, stream, branch_copies, branch_buf, head_count, arrive)
            gained = (stream[p] * gain_ref[layer : layer + 1, :]).astype(BF16)
            if p == 0:
                load[layer, 0].wait()
                load[layer, 1].wait()
            lead_buf[layer, p, me_feat, :, :span] = jnp.dot(
                gained, query_w[layer, :, :span], preferred_element_type=F32
            ).astype(BF16)
            values = [jnp.sum(stream[p] * stream[p], axis=1, keepdims=True)]
            gained_wide = gained.astype(F32)
            gates = gate_w[layer].astype(F32)
            for h in range(heads):
                values.append(jnp.sum(gained_wide * gates[h : h + 1, :], axis=1, keepdims=True))
            small = jnp.zeros((n, LANES), F32)
            for k, value in enumerate(values):
                spots = (lane == k) | (lane == fields + k) | (lane == 2 * fields + k)
                small = jnp.where(spots, value, small)
            high = small.astype(BF16).astype(F32)
            rest = small - high
            middle = rest.astype(BF16).astype(F32)
            lead_buf[layer, p, me_feat, :, span:] = jnp.where(
                lane < fields, high, jnp.where(lane < 2 * fields, middle, rest - middle)
            ).astype(BF16)
            own = lead_buf.at[layer, p, me_feat]
            lead_copies.append(exchange("feat", feat_count, me_feat, own, own))
            copies = []
            for h in range(1, heads):
                query_buf[layer, p, h - 1, me_feat] = jnp.dot(
                    gained, query_w[layer, :, h * span : (h + 1) * span], preferred_element_type=F32
                ).astype(BF16)
                own = query_buf.at[layer, p, h - 1, me_feat]
                copies.append(exchange("feat", feat_count, me_feat, own, own))
            query_copies.append(copies)
            for slot, weight in ((2, key_w), (3, value_w)):
                if p == 0:
                    load[layer, slot].wait()
                pair_buf[layer, p, me_feat, :, (slot - 2) * kv_columns : (slot - 1) * kv_columns] = (
                    jnp.dot(gained, weight[layer], preferred_element_type=F32).astype(BF16)
                )
            own = pair_buf.at[layer, p, me_feat]
            pair_copies.append(exchange("feat", feat_count, me_feat, own, own))

        query, decay, inverse, read_copies = [], [], [], []
        for p in range(parts):
            arrive(lead_copies[p])
            totals = lead_buf[layer, p, 0, :, span:].astype(F32)
            for i in range(1, feat_count):
                totals = totals + lead_buf[layer, p, i, :, span:].astype(F32)
            totals = (
                totals
                + pltpu.roll(totals, LANES - fields, 1)
                + pltpu.roll(totals, LANES - 2 * fields, 1)
            )
            inverse.append(lax.rsqrt(totals[:, :1] / (width * feat_count) + 1e-06))
            gate = totals[:, 1 : 1 + heads] * inverse[p] + bias_ref[layer : layer + 1, :]
            decay.append(1.0 / (1.0 + jnp.exp(gate)))
            query.append([])
            read_copies.append([])
            for h in range(heads):
                if h == 0:
                    summed = lead_buf[layer, p, 0, :, :span].astype(F32)
                    for i in range(1, feat_count):
                        summed = summed + lead_buf[layer, p, i, :, :span].astype(F32)
                else:
                    arrive(query_copies[p][h - 1])
                    summed = query_buf[layer, p, h - 1, 0].astype(F32)
                    for i in range(1, feat_count):
                        summed = summed + query_buf[layer, p, h - 1, i].astype(F32)
                summed = summed * inverse[p]
                rows = [summed[:, i * head_size : (i + 1) * head_size] for i in range(group)]
                stacked = jnp.concatenate(rows, axis=0).astype(BF16)
                query[p].append([row.astype(BF16).astype(F32) for row in rows])
                for start in range(0, block, 256):
                    stop = min(start + 256, block)
                    left = jnp.dot(stacked, left_sel[:, start:stop], preferred_element_type=F32)
                    right = jnp.dot(stacked, right_sel[:, start:stop], preferred_element_type=F32)
                    value = left * right * pair_scale[:, start:stop]
                    for lo in range(start, stop, LANES):
                        hi = min(lo + LANES, stop)
                        phi[lo // LANES, : group * n, : hi - lo] = value[:, lo - start : hi - start]

                def read(step, carry, h=h, p=p):
                    if h == 0:
                        for extra in range(unroll):
                            r = p * n + step * unroll + extra
                            pltpu.make_async_copy(
                                retained_hbm.at[layer, r], state.at[layer, r], state_sem.at[layer, r]
                            ).wait()
                    for extra in range(unroll):
                        i = step * unroll + extra
                        at = pl.ds(i, 8, stride=n)
                        lhs = jnp.concatenate(
                            [phi[c, at, :] for c in range(phi.shape[0])], axis=1
                        )[:, :block]
                        history[at, :] = jnp.dot(
                            lhs.astype(BF16), state[layer, p * n + i, h], preferred_element_type=F32
                        )
                    return carry

                lax.fori_loop(0, n // unroll, read, 0)
                read_buf[layer, p, h, me_feat] = history[: group * n, :].astype(BF16)
                own = read_buf.at[layer, p, h, me_feat]
                read_copies[p].append(exchange("feat", feat_count, me_feat, own, own))

        for p in range(parts):
            arrive(pair_copies[p])
            summed = pair_buf[layer, p, 0].astype(F32)
            for i in range(1, feat_count):
                summed = summed + pair_buf[layer, p, i].astype(F32)
            summed = (summed * inverse[p]).astype(BF16).astype(F32)
            if p == 0:
                load[layer, 4].wait()
            branch_copies[p] = []
            partial = None
            for h in range(heads):
                key = summed[:, h * head_size : (h + 1) * head_size]
                value = summed[:, kv_columns + h * head_size : kv_columns + (h + 1) * head_size]
                cross = []
                for i in range(group):
                    along = jnp.sum(query[p][h][i] * key, axis=1, keepdims=True)
                    cross.append(along * along / head_size)
                arrive(read_copies[p][h])
                reads = read_buf[layer, p, h, 0].astype(F32)
                for i in range(1, feat_count):
                    reads = reads + read_buf[layer, p, h, i].astype(F32)
                mixed = []
                for i in range(group):
                    readout = (
                        decay[p][:, h : h + 1] * reads[i * n : (i + 1) * n] + cross[i] * value
                    )
                    scale = lax.rsqrt(jnp.mean(readout * readout, axis=1, keepdims=True) + 1e-06)
                    mixed.append((readout * scale * read_ref[layer : layer + 1, :]).astype(BF16))
                mixed = jnp.concatenate(mixed, axis=1)
                pieces = []
                for c in range(chunks):
                    part = jnp.dot(
                        mixed,
                        out_w[layer, h * span : (h + 1) * span, c * chunk : (c + 1) * chunk],
                        preferred_element_type=F32,
                    )
                    if h > 0:
                        part = part + partial[c]
                    pieces.append(part)
                    if h == heads - 1:
                        branch_buf[layer, p, c, me_head] = part.astype(BF16)
                        own = branch_buf.at[layer, p, c, me_head]
                        branch_copies[p].append(exchange("head", head_count, me_head, own, own))
                partial = pieces

    for p in range(parts):
        done = finish(p, layers - 1, stream, branch_copies, branch_buf, head_count, arrive)
        result_ref[p * n : (p + 1) * n, :] = done.astype(BF16)
    for copy in sent:
        copy.wait_send()


def finish(p, layer, stream, branch_copies, branch_buf, head_count, arrive):
    branch = []
    for c in range(len(branch_copies[p])):
        arrive(branch_copies[p][c])
        total = branch_buf[layer, p, c, 0].astype(F32)
        for i in range(1, head_count):
            total = total + branch_buf[layer, p, c, i].astype(F32)
        branch.append(total)
    branch = jnp.concatenate(branch, axis=1) if len(branch) > 1 else branch[0]
    return (stream[p] + branch).astype(BF16).astype(F32)


def body(
    feat_count,
    head_count,
    token_ids,
    embedding,
    retained,
    query_weight,
    key_weight,
    value_weight,
    gate_weight,
    gate_bias,
    norm_gain,
    read_gain,
    out_weight,
):
    layers, requests, heads, block, head_size = retained.shape
    width = query_weight.shape[1]
    query_columns = query_weight.shape[2]
    kv_columns = key_weight.shape[2]
    group = query_columns // (heads * head_size)
    span = group * head_size
    parts = 2 if requests % 16 == 0 else 1
    n = requests // parts
    chunks = 1
    copies = parts * (
        (head_count - 1)
        + layers * ((1 + 2 * heads) * (feat_count - 1) + chunks * (head_count - 1))
    )
    gate_rows = jnp.swapaxes(gate_weight, 1, 2)
    window = 16
    picked = pl.pallas_call(
        lookup,
        out_shape=pltpu.VMEM((requests, width), BF16),
        in_specs=[pl.BlockSpec(memory_space=pltpu.SMEM), pl.BlockSpec(memory_space=pl.ANY)],
        out_specs=pl.BlockSpec(memory_space=pltpu.VMEM),
        scratch_shapes=[
            pltpu.VMEM((requests * window, width), BF16),
            pltpu.SemaphoreType.DMA((requests,)),
        ],
    )(token_ids, embedding)
    anywhere = pl.BlockSpec(memory_space=pl.ANY)
    local = pl.BlockSpec(memory_space=pltpu.VMEM)
    return pl.pallas_call(
        functools.partial(kernel, feat_count, head_count, parts),
        out_shape=pltpu.VMEM((requests, width), BF16),
        in_specs=[local] + [anywhere] * 9,
        out_specs=local,
        scratch_shapes=[
            pltpu.VMEM(retained.shape, BF16),
            pltpu.VMEM(query_weight.shape, BF16),
            pltpu.VMEM(key_weight.shape, BF16),
            pltpu.VMEM(value_weight.shape, BF16),
            pltpu.VMEM(gate_rows.shape, BF16),
            pltpu.VMEM(gate_bias.shape, F32),
            pltpu.VMEM(norm_gain.shape, F32),
            pltpu.VMEM(read_gain.shape, F32),
            pltpu.VMEM(out_weight.shape, BF16),
            pltpu.VMEM((parts, head_count, n, width), BF16),
            pltpu.VMEM((layers, parts, feat_count, n, span + LANES), BF16),
            pltpu.VMEM((layers, parts, max(heads - 1, 1), feat_count, n, span), BF16),
            pltpu.VMEM((layers, parts, feat_count, n, 2 * kv_columns), BF16),
            pltpu.VMEM((layers, parts, heads, feat_count, n * group, head_size), BF16),
            pltpu.VMEM((layers, parts, chunks, head_count, n, width // chunks), BF16),
            pltpu.VMEM((head_size, block), BF16),
            pltpu.VMEM((head_size, block), BF16),
            pltpu.VMEM((1, block), F32),
            pltpu.VMEM((pl.cdiv(block, LANES), 8 * n, LANES), F32),
            pltpu.VMEM((8 * n, head_size), F32),
            pltpu.SemaphoreType.DMA((layers, 8)),
            pltpu.SemaphoreType.DMA((layers, requests)),
            pltpu.SemaphoreType.DMA((copies,)),
            pltpu.SemaphoreType.DMA((copies,)),
        ],
        compiler_params=pltpu.CompilerParams(
            collective_id=0, has_side_effects=True, vmem_limit_bytes=66_000_000
        ),
    )(
        pltpu.with_memory_space_constraint(picked, pltpu.VMEM),
        retained,
        query_weight,
        key_weight,
        value_weight,
        gate_rows,
        gate_bias,
        norm_gain,
        read_gain,
        out_weight,
    )


def solution(mesh):
    return jax.shard_map(
        functools.partial(body, mesh.shape["feat"], mesh.shape["head"]),
        mesh=mesh,
        in_specs=(
            P("groups"),
            P("head", "feat"),
            P(None, "groups", "head", "feat", None),
            P(None, "feat", "head"),
            P(None, "feat", "head"),
            P(None, "feat", "head"),
            P(None, "feat", "head"),
            P(None, "head"),
            P(None, "feat"),
            P(),
            P(None, "head", "feat"),
        ),
        out_specs=P("groups", "feat"),
        check_vma=False,
    )
```

```python
import functools
import math

import jax
import jax.numpy as jnp
from jax import lax
from jax.experimental import pallas as pl
from jax.experimental.pallas import tpu as pltpu
from jax.sharding import PartitionSpec as P

MESH = pl.DeviceIdType.MESH
F32 = jnp.float32
BF16 = jnp.bfloat16
LANES = 128


def lookup(ids_ref, table_hbm, picked_ref, rows_buf, row_sem):
    requests, width = picked_ref.shape
    table_rows = table_hbm.shape[0]
    base = lax.axis_index("head") * table_rows
    window = rows_buf.shape[0] // requests
    out_row = lax.broadcasted_iota(jnp.int32, (requests, requests * window), 0)
    column = lax.broadcasted_iota(jnp.int32, (requests, requests * window), 1)
    select = jnp.zeros((requests, requests * window), F32)
    copies = []
    for i in range(requests):
        local = ids_ref[i] - base
        row = jnp.clip(local, 0, table_rows - 1)
        first = pl.multiple_of(jnp.minimum((row // 8) * 8, table_rows - window), 8)
        copy = pltpu.make_async_copy(
            table_hbm.at[pl.ds(first, window)],
            rows_buf.at[pl.ds(i * window, window)],
            row_sem.at[i],
        )
        copy.start()
        copies.append(copy)
        value = jnp.where(local == row, 1.0, 0.0)
        hit = (out_row == i) & (column == i * window + row - first)
        select = jnp.where(hit, value, select)
    for copy in copies:
        copy.wait()
    picked_ref[...] = jnp.dot(
        select.astype(BF16), rows_buf[...], preferred_element_type=F32
    ).astype(BF16)


def partner_of(me, count, turn):
    if count == 4:
        return (3 - me, lax.rem(me + 2, 4), me + 1 - 2 * lax.rem(me, 2))[turn - 1]
    return lax.rem(me + turn, count)


def kernel(
    feat_count,
    head_count,
    parts,
    picked_ref,
    retained_hbm,
    query_hbm,
    key_hbm,
    value_hbm,
    gate_hbm,
    bias_hbm,
    gain_hbm,
    read_hbm,
    out_hbm,
    result_ref,
    state,
    query_w,
    key_w,
    value_w,
    gate_w,
    bias_ref,
    gain_ref,
    read_ref,
    out_w,
    pick_buf,
    lead_buf,
    query_buf,
    pair_buf,
    read_buf,
    branch_buf,
    left_at,
    right_at,
    pair_scale,
    phi,
    history,
    load_sem,
    state_sem,
    send_sem,
    recv_sem,
    reach_sem,
):
    layers, requests, heads, block, head_size = state.shape
    width = query_w.shape[1]
    query_columns = query_w.shape[2]
    kv_columns = key_w.shape[2]
    chunks, chunk = branch_buf.shape[2], branch_buf.shape[5]
    group = query_columns // (heads * head_size)
    span = group * head_size
    n = requests // parts
    me_feat = lax.axis_index("feat")
    me_head = lax.axis_index("head")

    last = feat_count - 1
    barrier = pltpu.get_barrier_semaphore()
    for d in range(1, head_count):
        pl.semaphore_signal(
            barrier, inc=1, device_id={"head": lax.rem(me_head + d, head_count)}, device_id_type=MESH
        )

    def tell(semaphore, condition, other):
        @pl.when(condition)
        def _():
            pl.semaphore_signal(semaphore, inc=1, device_id={"feat": other}, device_id_type=MESH)

    def hear(semaphore, condition):
        @pl.when(condition)
        def _():
            pl.semaphore_wait(semaphore, 1)

    tell(barrier, me_feat > 0, me_feat - 1)
    tell(barrier, me_feat < last, me_feat + 1)

    load = {}

    def start_load(slot, source, target, layer):
        load[layer, slot] = pltpu.make_async_copy(source, target, load_sem.at[layer, slot])
        load[layer, slot].start()

    def load_inputs(layer):
        pairs = [(gate_hbm, gate_w), (query_hbm, query_w), (key_hbm, key_w), (value_hbm, value_w)]
        for slot, (source, target) in enumerate(pairs):
            start_load(slot, source.at[layer], target.at[layer], layer)

    def load_state(layer):
        for r in range(requests):
            pltpu.make_async_copy(
                retained_hbm.at[layer, r], state.at[layer, r], state_sem.at[layer, r]
            ).start()
        start_load(4, out_hbm.at[layer], out_w.at[layer], layer)

    start_load(5, gain_hbm, gain_ref, 0)
    start_load(6, bias_hbm, bias_ref, 0)
    start_load(7, read_hbm, read_ref, 0)
    load_inputs(0)
    neighbours = jnp.minimum(me_feat, 1) + jnp.minimum(last - me_feat, 1)
    pl.semaphore_wait(barrier, head_count - 1 + neighbours)

    used = [0]
    sent = []

    def exchange(axis, count, me, source, slots):
        number = used[0]
        used[0] += 1
        for d in range(1, count):
            pltpu.make_async_remote_copy(
                src_ref=source,
                dst_ref=slots.at[me],
                send_sem=send_sem.at[number],
                recv_sem=recv_sem.at[number],
                device_id={axis: partner_of(me, count, d)},
                device_id_type=MESH,
            ).start()
        others = slots.at[pl.ds(0, count - 1)]
        sent.append(pltpu.make_async_copy(others, others, send_sem.at[number]))
        return pltpu.make_async_copy(others, others, recv_sem.at[number])

    def drain():
        while sent:
            sent.pop(0).wait()

    pick_copies = []
    for p in range(parts):
        rows = slice(p * n, (p + 1) * n)
        pick_copies.append(
            exchange(
                "head", head_count, me_head, picked_ref.at[rows], pick_buf.at[p]
            )
        )
    tell(reach_sem.at[0], (me_feat == 1) & (me_feat < last), me_feat + 1)
    tell(reach_sem.at[1], (me_feat == last - 1) & (me_feat > 0), me_feat - 1)
    load_state(0)
    for layer in range(1, layers):
        load_inputs(layer)
        load_state(layer)

    position = lax.broadcasted_iota(jnp.int32, (head_size, LANES), 0)
    begin = position * head_size - (position * (position - 1)) // 2 - me_feat * block
    offset = lax.broadcasted_iota(jnp.int32, (n, LANES), 1)
    for c in range(left_at.shape[0]):
        reached = jnp.where(begin - lax.broadcasted_iota(jnp.int32, begin.shape, 1) <= c * LANES, 1, 0)
        first = jnp.sum(reached, axis=0, keepdims=True) - 1
        first = jnp.broadcast_to(first, (n, LANES))
        start = first * head_size - (first * (first - 1)) // 2 - me_feat * block
        second = jnp.minimum(offset + c * LANES - start + first, head_size - 1)
        left_at[c] = first
        right_at[c] = second
        pair_scale[c] = jnp.where(first == second, 1.0, math.sqrt(2.0)).astype(F32)
    phi[...] = jnp.zeros(phi.shape, F32)

    for slot in (5, 6, 7):
        load[0, slot].wait()

    hear(reach_sem.at[0], me_feat >= 2)
    tell(reach_sem.at[0], (me_feat >= 2) & (me_feat < last), me_feat + 1)
    hear(reach_sem.at[1], me_feat <= last - 2)
    tell(reach_sem.at[1], (me_feat <= last - 2) & (me_feat > 0), me_feat - 1)

    fields = heads + 1
    lane = lax.broadcasted_iota(jnp.int32, (n, LANES), 1)
    unroll = 4 if n % 4 == 0 else 1
    stream = [None] * parts
    branch_copies = [None] * parts

    for p in range(parts):
        pick_buf[p, me_head] = picked_ref[p * n : (p + 1) * n, :]

    for layer in range(layers):
        lead_copies, query_copies, gained_all = [], [], []
        for p in range(parts):
            if p == 0:
                drain()
            if layer == 0:
                pick_copies[p].wait()
                total = pick_buf[p, 0].astype(F32)
                for i in range(1, head_count):
                    total = total + pick_buf[p, i].astype(F32)
                stream[p] = total
            else:
                stream[p] = finish(p, layer - 1, stream, branch_copies, branch_buf, head_count)
            gained = (stream[p] * gain_ref[layer : layer + 1, :]).astype(BF16)
            if p == 0:
                load[layer, 0].wait()
                load[layer, 1].wait()
            lead_buf[layer, p, me_feat, :, :span] = jnp.dot(
                gained, query_w[layer, :, :span], preferred_element_type=F32
            ).astype(BF16)
            values = [jnp.sum(stream[p] * stream[p], axis=1, keepdims=True)]
            gained_wide = gained.astype(F32)
            gates = gate_w[layer].astype(F32)
            for h in range(heads):
                values.append(jnp.sum(gained_wide * gates[h : h + 1, :], axis=1, keepdims=True))
            small = jnp.zeros((n, LANES), F32)
            for k, value in enumerate(values):
                spots = (lane == k) | (lane == fields + k) | (lane == 2 * fields + k)
                small = jnp.where(spots, value, small)
            high = small.astype(BF16).astype(F32)
            rest = small - high
            middle = rest.astype(BF16).astype(F32)
            lead_buf[layer, p, me_feat, :, span:] = jnp.where(
                lane < fields, high, jnp.where(lane < 2 * fields, middle, rest - middle)
            ).astype(BF16)
            slots = lead_buf.at[layer, p]
            lead_copies.append(exchange("feat", feat_count, me_feat, slots.at[me_feat], slots))
            copies = []
            for h in range(1, heads):
                query_buf[layer, p, h - 1, me_feat] = jnp.dot(
                    gained, query_w[layer, :, h * span : (h + 1) * span], preferred_element_type=F32
                ).astype(BF16)
                slots = query_buf.at[layer, p, h - 1]
                copies.append(exchange("feat", feat_count, me_feat, slots.at[me_feat], slots))
            query_copies.append(copies)
            gained_all.append(gained)
        gained = jnp.concatenate(gained_all, axis=0)
        for slot, weight in ((2, key_w), (3, value_w)):
            load[layer, slot].wait()
            pair_buf[layer, me_feat, :, (slot - 2) * kv_columns : (slot - 1) * kv_columns] = jnp.dot(
                gained, weight[layer], preferred_element_type=F32
            ).astype(BF16)
        slots = pair_buf.at[layer]
        pair_copies = exchange("feat", feat_count, me_feat, slots.at[me_feat], slots)

        query, decay, inverse, read_copies = [], [], [], []
        for p in range(parts):
            lead_copies[p].wait()
            totals = lead_buf[layer, p, 0, :, span:].astype(F32)
            for i in range(1, feat_count):
                totals = totals + lead_buf[layer, p, i, :, span:].astype(F32)
            totals = (
                totals
                + pltpu.roll(totals, LANES - fields, 1)
                + pltpu.roll(totals, LANES - 2 * fields, 1)
            )
            inverse.append(lax.rsqrt(totals[:, :1] / (width * feat_count) + 1e-06))
            gate = totals[:, 1 : 1 + heads] * inverse[p] + bias_ref[layer : layer + 1, :]
            decay.append(1.0 / (1.0 + jnp.exp(gate)))
            query.append([])
            read_copies.append([])

            def features(h):
                if h == 0:
                    summed = lead_buf[layer, p, 0, :, :span].astype(F32)
                    for i in range(1, feat_count):
                        summed = summed + lead_buf[layer, p, i, :, :span].astype(F32)
                else:
                    query_copies[p][h - 1].wait()
                    summed = query_buf[layer, p, h - 1, 0].astype(F32)
                    for i in range(1, feat_count):
                        summed = summed + query_buf[layer, p, h - 1, i].astype(F32)
                summed = (summed * inverse[p]).astype(BF16).astype(F32)
                rows = [summed[:, i * head_size : (i + 1) * head_size] for i in range(group)]
                query[p].append(rows)
                for c in range(left_at.shape[0]):
                    first, second, scale = left_at[c], right_at[c], pair_scale[c]
                    for i, row in enumerate(rows):
                        left = jnp.take_along_axis(row, first, axis=1)
                        right = jnp.take_along_axis(row, second, axis=1)
                        phi[h % 2, c, i * n : (i + 1) * n, :] = left * right * scale

            features(0)
            for h in range(heads):
                for step in range(n // unroll):
                    if h == 0:
                        for extra in range(unroll):
                            r = p * n + step * unroll + extra
                            pltpu.make_async_copy(
                                retained_hbm.at[layer, r], state.at[layer, r], state_sem.at[layer, r]
                            ).wait()
                    if h + 1 < heads and step == n // unroll - 1:
                        features(h + 1)
                    for extra in range(unroll):
                        i = step * unroll + extra
                        at = pl.ds(i, 8, stride=n)
                        lhs = jnp.concatenate(
                            [phi[h % 2, c, at, :] for c in range(phi.shape[1])], axis=1
                        )[:, :block]
                        history[at, :] = jnp.dot(
                            lhs.astype(BF16), state[layer, p * n + i, h], preferred_element_type=F32
                        )
                read_buf[layer, p, h, me_feat] = history[: group * n, :].astype(BF16)
                slots = read_buf.at[layer, p, h]
                read_copies[p].append(
                    exchange("feat", feat_count, me_feat, slots.at[me_feat], slots)
                )

        for p in range(parts):
            if p == 0:
                pair_copies.wait()
            rows = slice(p * n, (p + 1) * n)
            summed = pair_buf[layer, 0, rows].astype(F32)
            for i in range(1, feat_count):
                summed = summed + pair_buf[layer, i, rows].astype(F32)
            summed = (summed * inverse[p]).astype(BF16).astype(F32)
            if p == 0:
                load[layer, 4].wait()
            branch_copies[p] = []
            partial = None
            for h in range(heads):
                key = summed[:, h * head_size : (h + 1) * head_size]
                value = summed[:, kv_columns + h * head_size : kv_columns + (h + 1) * head_size]
                cross = []
                for i in range(group):
                    along = jnp.sum(query[p][h][i] * key, axis=1, keepdims=True)
                    cross.append(along * along / head_size)
                read_copies[p][h].wait()
                reads = read_buf[layer, p, h, 0].astype(F32)
                for i in range(1, feat_count):
                    reads = reads + read_buf[layer, p, h, i].astype(F32)
                mixed = []
                for i in range(group):
                    readout = (
                        decay[p][:, h : h + 1] * reads[i * n : (i + 1) * n] + cross[i] * value
                    )
                    scale = lax.rsqrt(jnp.mean(readout * readout, axis=1, keepdims=True) + 1e-06)
                    mixed.append((readout * scale * read_ref[layer : layer + 1, :]).astype(BF16))
                mixed = jnp.concatenate(mixed, axis=1)
                pieces = []
                for c in range(chunks):
                    part = jnp.dot(
                        mixed,
                        out_w[layer, h * span : (h + 1) * span, c * chunk : (c + 1) * chunk],
                        preferred_element_type=F32,
                    )
                    if h > 0:
                        part = part + partial[c]
                    pieces.append(part)
                    if h == heads - 1:
                        branch_buf[layer, p, c, me_head] = part.astype(BF16)
                        slots = branch_buf.at[layer, p, c]
                        branch_copies[p].append(
                            exchange("head", head_count, me_head, slots.at[me_head], slots)
                        )
                partial = pieces

    for p in range(parts):
        done = finish(p, layers - 1, stream, branch_copies, branch_buf, head_count)
        result_ref[p * n : (p + 1) * n, :] = done.astype(BF16)
    drain()


def finish(p, layer, stream, branch_copies, branch_buf, head_count):
    branch = []
    for c in range(len(branch_copies[p])):
        branch_copies[p][c].wait()
        total = branch_buf[layer, p, c, 0].astype(F32)
        for i in range(1, head_count):
            total = total + branch_buf[layer, p, c, i].astype(F32)
        branch.append(total)
    branch = jnp.concatenate(branch, axis=1) if len(branch) > 1 else branch[0]
    return (stream[p] + branch).astype(BF16).astype(F32)


def body(
    feat_count,
    head_count,
    token_ids,
    embedding,
    retained,
    query_weight,
    key_weight,
    value_weight,
    gate_weight,
    gate_bias,
    norm_gain,
    read_gain,
    out_weight,
):
    layers, requests, heads, block, head_size = retained.shape
    width = query_weight.shape[1]
    query_columns = query_weight.shape[2]
    kv_columns = key_weight.shape[2]
    group = query_columns // (heads * head_size)
    span = group * head_size
    parts = 2 if requests % 16 == 0 else 1
    n = requests // parts
    chunks = 2 if width % 256 == 0 else 1
    copies = parts + layers * (1 + parts * (2 * heads + chunks))
    gate_rows = jnp.swapaxes(gate_weight, 1, 2)
    window = 16
    picked = pl.pallas_call(
        lookup,
        out_shape=pltpu.VMEM((requests, width), BF16),
        in_specs=[pl.BlockSpec(memory_space=pltpu.SMEM), pl.BlockSpec(memory_space=pl.ANY)],
        out_specs=pl.BlockSpec(memory_space=pltpu.VMEM),
        scratch_shapes=[
            pltpu.VMEM((requests * window, width), BF16),
            pltpu.SemaphoreType.DMA((requests,)),
        ],
    )(token_ids, embedding)
    anywhere = pl.BlockSpec(memory_space=pl.ANY)
    local = pl.BlockSpec(memory_space=pltpu.VMEM)
    return pl.pallas_call(
        functools.partial(kernel, feat_count, head_count, parts),
        out_shape=pltpu.VMEM((requests, width), BF16),
        in_specs=[local] + [anywhere] * 9,
        out_specs=local,
        scratch_shapes=[
            pltpu.VMEM(retained.shape, BF16),
            pltpu.VMEM(query_weight.shape, BF16),
            pltpu.VMEM(key_weight.shape, BF16),
            pltpu.VMEM(value_weight.shape, BF16),
            pltpu.VMEM(gate_rows.shape, BF16),
            pltpu.VMEM(gate_bias.shape, F32),
            pltpu.VMEM(norm_gain.shape, F32),
            pltpu.VMEM(read_gain.shape, F32),
            pltpu.VMEM(out_weight.shape, BF16),
            pltpu.VMEM((parts, head_count, n, width), BF16),
            pltpu.VMEM((layers, parts, feat_count, n, span + LANES), BF16),
            pltpu.VMEM((layers, parts, max(heads - 1, 1), feat_count, n, span), BF16),
            pltpu.VMEM((layers, feat_count, requests, 2 * kv_columns), BF16),
            pltpu.VMEM((layers, parts, heads, feat_count, n * group, head_size), BF16),
            pltpu.VMEM((layers, parts, chunks, head_count, n, width // chunks), BF16),
            pltpu.VMEM((pl.cdiv(block, LANES), n, LANES), jnp.int32),
            pltpu.VMEM((pl.cdiv(block, LANES), n, LANES), jnp.int32),
            pltpu.VMEM((pl.cdiv(block, LANES), n, LANES), F32),
            pltpu.VMEM((2, pl.cdiv(block, LANES), 8 * n, LANES), F32),
            pltpu.VMEM((8 * n, head_size), F32),
            pltpu.SemaphoreType.DMA((layers, 8)),
            pltpu.SemaphoreType.DMA((layers, requests)),
            pltpu.SemaphoreType.DMA((copies,)),
            pltpu.SemaphoreType.DMA((copies,)),
            pltpu.SemaphoreType.REGULAR((2,)),
        ],
        compiler_params=pltpu.CompilerParams(
            collective_id=0, has_side_effects=True, vmem_limit_bytes=66_000_000
        ),
    )(
        pltpu.with_memory_space_constraint(picked, pltpu.VMEM),
        retained,
        query_weight,
        key_weight,
        value_weight,
        gate_rows,
        gate_bias,
        norm_gain,
        read_gain,
        out_weight,
    )


def solution(mesh):
    return jax.shard_map(
        functools.partial(body, mesh.shape["feat"], mesh.shape["head"]),
        mesh=mesh,
        in_specs=(
            P("groups"),
            P("head", "feat"),
            P(None, "groups", "head", "feat", None),
            P(None, "feat", "head"),
            P(None, "feat", "head"),
            P(None, "feat", "head"),
            P(None, "feat", "head"),
            P(None, "head"),
            P(None, "feat"),
            P(),
            P(None, "head", "feat"),
        ),
        out_specs=P("groups", "feat"),
        check_vma=False,
    )
```

```python
import functools
import math

import jax
import jax.numpy as jnp
from jax import lax
from jax.experimental import pallas as pl
from jax.experimental.pallas import tpu as pltpu
from jax.sharding import PartitionSpec as P

MESH = pl.DeviceIdType.MESH
F32 = jnp.float32
BF16 = jnp.bfloat16
LANES = 128


def partner_of(me, count, turn):
    if count == 4:
        return (3 - me, lax.rem(me + 2, 4), me + 1 - 2 * lax.rem(me, 2))[turn - 1]
    return lax.rem(me + turn, count)


def kernel(
    feat_count,
    head_count,
    parts,
    table_rows,
    ids_hbm,
    picked_ref,
    retained_hbm,
    query_hbm,
    key_hbm,
    value_hbm,
    gate_hbm,
    bias_hbm,
    gain_hbm,
    read_hbm,
    out_hbm,
    result_ref,
    ids_ref,
    state,
    query_w,
    key_w,
    value_w,
    gate_w,
    bias_ref,
    gain_ref,
    read_ref,
    out_w,
    pick_buf,
    lead_buf,
    query_buf,
    pair_buf,
    read_buf,
    branch_buf,
    left_at,
    right_at,
    pair_scale,
    phi,
    history,
    load_sem,
    state_sem,
    send_sem,
    recv_sem,
    reach_sem,
):
    layers, requests, heads, block, head_size = state.shape
    width = query_w.shape[1]
    query_columns = query_w.shape[2]
    chunks, chunk = branch_buf.shape[2], branch_buf.shape[5]
    group = query_columns // (heads * head_size)
    span = group * head_size
    n = requests // parts
    me_feat = lax.axis_index("feat")
    me_head = lax.axis_index("head")

    last = feat_count - 1
    barrier = pltpu.get_barrier_semaphore()
    for d in range(1, head_count):
        pl.semaphore_signal(
            barrier, inc=1, device_id={"head": lax.rem(me_head + d, head_count)}, device_id_type=MESH
        )

    def tell(semaphore, condition, other):
        @pl.when(condition)
        def _():
            pl.semaphore_signal(semaphore, inc=1, device_id={"feat": other}, device_id_type=MESH)

    def hear(semaphore, condition):
        @pl.when(condition)
        def _():
            pl.semaphore_wait(semaphore, 1)

    tell(barrier, me_feat > 0, me_feat - 1)
    tell(barrier, me_feat < last, me_feat + 1)

    load = {}

    def start_load(slot, source, target, layer):
        load[layer, slot] = pltpu.make_async_copy(source, target, load_sem.at[layer, slot])
        load[layer, slot].start()

    def load_inputs(layer):
        pairs = [(gate_hbm, gate_w), (query_hbm, query_w), (key_hbm, key_w), (value_hbm, value_w)]
        for slot, (source, target) in enumerate(pairs):
            start_load(slot, source.at[layer], target.at[layer], layer)

    def load_state(layer):
        for r in range(requests):
            pltpu.make_async_copy(
                retained_hbm.at[layer, r], state.at[layer, r], state_sem.at[layer, r]
            ).start()
        start_load(4, out_hbm.at[layer], out_w.at[layer], layer)

    start_load(8, ids_hbm, ids_ref, 0)
    start_load(5, gain_hbm, gain_ref, 0)
    start_load(6, bias_hbm, bias_ref, 0)
    start_load(7, read_hbm, read_ref, 0)
    load_inputs(0)
    neighbours = jnp.minimum(me_feat, 1) + jnp.minimum(last - me_feat, 1)
    pl.semaphore_wait(barrier, head_count - 1 + neighbours)

    used = [0]
    sent = []

    def exchange(axis, count, me, source, slots):
        number = used[0]
        used[0] += 1
        for d in range(1, count):
            pltpu.make_async_remote_copy(
                src_ref=source,
                dst_ref=slots.at[me],
                send_sem=send_sem.at[number],
                recv_sem=recv_sem.at[number],
                device_id={axis: partner_of(me, count, d)},
                device_id_type=MESH,
            ).start()
        others = slots.at[pl.ds(0, count - 1)]
        sent.append(pltpu.make_async_copy(others, others, send_sem.at[number]).wait)
        return pltpu.make_async_copy(others, others, recv_sem.at[number])

    def collect(axis, count, me, owner, slots):
        number = used[0]
        used[0] += 1
        mine = slots.at[me]
        others = slots.at[pl.ds(0, count - 1)]

        @pl.when(me != owner)
        def _():
            pltpu.make_async_remote_copy(
                src_ref=mine,
                dst_ref=mine,
                send_sem=send_sem.at[number],
                recv_sem=recv_sem.at[number],
                device_id={axis: owner},
                device_id_type=MESH,
            ).start()

        def finished():
            @pl.when(me != owner)
            def _():
                pltpu.make_async_copy(mine, mine, send_sem.at[number]).wait()

        sent.append(finished)
        return pltpu.make_async_copy(others, others, recv_sem.at[number])

    def drain(number):
        for _ in range(number):
            sent.pop(0)()

    pick_copies = []
    for p in range(parts):
        rows = slice(p * n, (p + 1) * n)
        pick_copies.append(
            exchange(
                "head", head_count, me_head, picked_ref.at[rows], pick_buf.at[p]
            )
        )
    tell(reach_sem.at[0], (me_feat == 1) & (me_feat < last), me_feat + 1)
    tell(reach_sem.at[1], (me_feat == last - 1) & (me_feat > 0), me_feat - 1)
    load_state(0)
    for layer in range(1, layers):
        load_inputs(layer)
        load_state(layer)

    position = lax.broadcasted_iota(jnp.int32, (head_size, LANES), 0)
    begin = position * head_size - (position * (position - 1)) // 2 - me_feat * block
    offset = lax.broadcasted_iota(jnp.int32, (n, LANES), 1)
    for c in range(left_at.shape[0]):
        reached = jnp.where(begin - lax.broadcasted_iota(jnp.int32, begin.shape, 1) <= c * LANES, 1, 0)
        first = jnp.sum(reached, axis=0, keepdims=True) - 1
        first = jnp.broadcast_to(first, (n, LANES))
        start = first * head_size - (first * (first - 1)) // 2 - me_feat * block
        second = jnp.minimum(offset + c * LANES - start + first, head_size - 1)
        left_at[c] = first
        right_at[c] = second
        pair_scale[c] = jnp.where(first == second, 1.0, math.sqrt(2.0)).astype(F32)
    phi[...] = jnp.zeros(phi.shape, F32)

    for slot in (5, 6, 7, 8):
        load[0, slot].wait()

    hear(reach_sem.at[0], me_feat >= 2)
    tell(reach_sem.at[0], (me_feat >= 2) & (me_feat < last), me_feat + 1)
    hear(reach_sem.at[1], me_feat <= last - 2)
    tell(reach_sem.at[1], (me_feat <= last - 2) & (me_feat > 0), me_feat - 1)

    fields = heads + 1
    owners = [(max(feat_count // 2, 1) - 1 + h) % feat_count for h in range(heads)]
    lane = lax.broadcasted_iota(jnp.int32, (n, LANES), 1)
    unroll = 4 if n % 4 == 0 else 1
    stream = [None] * parts
    branch_copies = [None] * parts

    for p in range(parts):
        pick_buf[p, me_head] = picked_ref[p * n : (p + 1) * n, :]

    for layer in range(layers):
        lead_copies, query_copies, pair_copies = [], [], []
        earlier = len(sent)
        for p in range(parts):
            if layer == 0:
                pick_copies[p].wait()
                token = jnp.zeros((n, 1), jnp.int32)
                line = lax.broadcasted_iota(jnp.int32, (n, 1), 0)
                for i in range(n):
                    token = jnp.where(line == i, ids_ref[p * n + i], token)
                total = jnp.zeros((n, width), F32)
                for i in range(head_count):
                    mine = (token >= i * table_rows) & (token < (i + 1) * table_rows)
                    total = jnp.where(mine, pick_buf[p, i].astype(F32), total)
                stream[p] = total
            else:
                stream[p] = finish(p, layer - 1, stream, branch_copies, branch_buf, head_count)
            gained = (stream[p] * gain_ref[layer : layer + 1, :]).astype(BF16)
            if p == 0:
                load[layer, 0].wait()
                load[layer, 1].wait()
            lead_buf[layer, p, me_feat, :, :span] = jnp.dot(
                gained, query_w[layer, :, :span], preferred_element_type=F32
            ).astype(BF16)
            values = [jnp.sum(stream[p] * stream[p], axis=1, keepdims=True)]
            gained_wide = gained.astype(F32)
            gates = gate_w[layer].astype(F32)
            for h in range(heads):
                values.append(jnp.sum(gained_wide * gates[h : h + 1, :], axis=1, keepdims=True))
            small = jnp.zeros((n, LANES), F32)
            for k, value in enumerate(values):
                spots = (lane == k) | (lane == fields + k) | (lane == 2 * fields + k)
                small = jnp.where(spots, value, small)
            high = small.astype(BF16).astype(F32)
            rest = small - high
            middle = rest.astype(BF16).astype(F32)
            lead_buf[layer, p, me_feat, :, span:] = jnp.where(
                lane < fields, high, jnp.where(lane < 2 * fields, middle, rest - middle)
            ).astype(BF16)
            slots = lead_buf.at[layer, p]
            lead_copies.append(exchange("feat", feat_count, me_feat, slots.at[me_feat], slots))
            copies = []
            for h in range(1, heads):
                query_buf[layer, p, h - 1, me_feat] = jnp.dot(
                    gained, query_w[layer, :, h * span : (h + 1) * span], preferred_element_type=F32
                ).astype(BF16)
                slots = query_buf.at[layer, p, h - 1]
                copies.append(exchange("feat", feat_count, me_feat, slots.at[me_feat], slots))
            query_copies.append(copies)
            for slot, weight in ((2, key_w), (3, value_w)):
                if p == 0:
                    load[layer, slot].wait()
                product = jnp.dot(gained, weight[layer], preferred_element_type=F32).astype(BF16)
                for h in range(heads):
                    pair_buf[layer, p, h, me_feat, :, (slot - 2) * head_size : (slot - 1) * head_size] = (
                        product[:, h * head_size : (h + 1) * head_size]
                    )
            pair_copies.append(
                [
                    collect("feat", feat_count, me_feat, owners[h], pair_buf.at[layer, p, h])
                    for h in range(heads)
                ]
            )

        drain(earlier)
        query, decay, inverse, read_copies = [], [], [], []
        for p in range(parts):
            lead_copies[p].wait()
            totals = lead_buf[layer, p, 0, :, span:].astype(F32)
            for i in range(1, feat_count):
                totals = totals + lead_buf[layer, p, i, :, span:].astype(F32)
            totals = (
                totals
                + pltpu.roll(totals, LANES - fields, 1)
                + pltpu.roll(totals, LANES - 2 * fields, 1)
            )
            inverse.append(lax.rsqrt(totals[:, :1] / (width * feat_count) + 1e-06))
            gate = totals[:, 1 : 1 + heads] * inverse[p] + bias_ref[layer : layer + 1, :]
            decay.append(1.0 / (1.0 + jnp.exp(gate)))
            query.append([])
            read_copies.append([])

            def features(h):
                if h == 0:
                    summed = lead_buf[layer, p, 0, :, :span].astype(F32)
                    for i in range(1, feat_count):
                        summed = summed + lead_buf[layer, p, i, :, :span].astype(F32)
                else:
                    query_copies[p][h - 1].wait()
                    summed = query_buf[layer, p, h - 1, 0].astype(F32)
                    for i in range(1, feat_count):
                        summed = summed + query_buf[layer, p, h - 1, i].astype(F32)
                summed = (summed * inverse[p]).astype(BF16).astype(F32)
                rows = [summed[:, i * head_size : (i + 1) * head_size] for i in range(group)]
                query[p].append(rows)
                for c in range(left_at.shape[0]):
                    first, second, scale = left_at[c], right_at[c], pair_scale[c]
                    for i, row in enumerate(rows):
                        left = jnp.take_along_axis(row, first, axis=1)
                        right = jnp.take_along_axis(row, second, axis=1)
                        phi[h % 2, c, i * n : (i + 1) * n, :] = left * right * scale

            features(0)
            for h in range(heads):
                for step in range(n // unroll):
                    if h == 0:
                        for extra in range(unroll):
                            r = p * n + step * unroll + extra
                            pltpu.make_async_copy(
                                retained_hbm.at[layer, r], state.at[layer, r], state_sem.at[layer, r]
                            ).wait()
                    if h + 1 < heads and step == n // unroll - 1:
                        features(h + 1)
                    for extra in range(unroll):
                        i = step * unroll + extra
                        at = pl.ds(i, 8, stride=n)
                        lhs = jnp.concatenate(
                            [phi[h % 2, c, at, :] for c in range(phi.shape[1])], axis=1
                        )[:, :block]
                        history[at, :] = jnp.dot(
                            lhs.astype(BF16), state[layer, p * n + i, h], preferred_element_type=F32
                        )
                kept = jnp.concatenate([decay[p][:, h : h + 1]] * group, axis=0)
                kept = kept * history[: group * n, :]

                @pl.when(me_feat != owners[h])
                def _():
                    read_buf[layer, p, h, me_feat] = kept.astype(BF16)

                @pl.when(me_feat == owners[h])
                def _():
                    pair_copies[p][h].wait()
                    summed = pair_buf[layer, p, h, 0].astype(F32)
                    for i in range(1, feat_count):
                        summed = summed + pair_buf[layer, p, h, i].astype(F32)
                    summed = (summed * inverse[p]).astype(BF16).astype(F32)
                    key, value = summed[:, :head_size], summed[:, head_size:]
                    fresh = []
                    for row in query[p][h]:
                        along = jnp.sum(row * key, axis=1, keepdims=True)
                        fresh.append(along * along / head_size * value)
                    fresh = jnp.concatenate(fresh, axis=0)
                    read_buf[layer, p, h, me_feat] = (kept + fresh).astype(BF16)

                slots = read_buf.at[layer, p, h]
                read_copies[p].append(
                    exchange("feat", feat_count, me_feat, slots.at[me_feat], slots)
                )

        for p in range(parts):
            if p == 0:
                load[layer, 4].wait()
            branch_copies[p] = []
            partial = None
            for h in range(heads):
                read_copies[p][h].wait()
                reads = read_buf[layer, p, h, 0].astype(F32)
                for i in range(1, feat_count):
                    reads = reads + read_buf[layer, p, h, i].astype(F32)
                mixed = []
                for i in range(group):
                    readout = reads[i * n : (i + 1) * n]
                    scale = lax.rsqrt(jnp.mean(readout * readout, axis=1, keepdims=True) + 1e-06)
                    mixed.append((readout * scale * read_ref[layer : layer + 1, :]).astype(BF16))
                mixed = jnp.concatenate(mixed, axis=1)
                pieces = []
                for c in range(chunks):
                    part = jnp.dot(
                        mixed,
                        out_w[layer, h * span : (h + 1) * span, c * chunk : (c + 1) * chunk],
                        preferred_element_type=F32,
                    )
                    if h > 0:
                        part = part + partial[c]
                    pieces.append(part)
                    if h == heads - 1:
                        branch_buf[layer, p, c, me_head] = part.astype(BF16)
                        slots = branch_buf.at[layer, p, c]
                        branch_copies[p].append(
                            exchange("head", head_count, me_head, slots.at[me_head], slots)
                        )
                partial = pieces

    for p in range(parts):
        done = finish(p, layers - 1, stream, branch_copies, branch_buf, head_count)
        result_ref[p * n : (p + 1) * n, :] = done.astype(BF16)
    drain(len(sent))


def finish(p, layer, stream, branch_copies, branch_buf, head_count):
    branch = []
    for c in range(len(branch_copies[p])):
        branch_copies[p][c].wait()
        total = branch_buf[layer, p, c, 0].astype(F32)
        for i in range(1, head_count):
            total = total + branch_buf[layer, p, c, i].astype(F32)
        branch.append(total)
    branch = jnp.concatenate(branch, axis=1) if len(branch) > 1 else branch[0]
    return (stream[p] + branch).astype(BF16).astype(F32)


def body(
    feat_count,
    head_count,
    token_ids,
    embedding,
    retained,
    query_weight,
    key_weight,
    value_weight,
    gate_weight,
    gate_bias,
    norm_gain,
    read_gain,
    out_weight,
):
    layers, requests, heads, block, head_size = retained.shape
    width = query_weight.shape[1]
    query_columns = query_weight.shape[2]
    group = query_columns // (heads * head_size)
    span = group * head_size
    parts = 2 if requests % 16 == 0 else 1
    n = requests // parts
    chunks = 2 if width % 256 == 0 else 1
    copies = parts + layers * parts * (3 * heads + chunks)
    gate_rows = jnp.swapaxes(gate_weight, 1, 2)
    local_row = token_ids - lax.axis_index("head") * embedding.shape[0]
    picked = lax.gather(
        embedding,
        local_row[:, None],
        lax.GatherDimensionNumbers(
            offset_dims=(1,), collapsed_slice_dims=(0,), start_index_map=(0,)
        ),
        slice_sizes=(1, width),
        mode=lax.GatherScatterMode.CLIP,
    )
    anywhere = pl.BlockSpec(memory_space=pl.ANY)
    local = pl.BlockSpec(memory_space=pltpu.VMEM)
    return pl.pallas_call(
        functools.partial(kernel, feat_count, head_count, parts, embedding.shape[0]),
        out_shape=pltpu.VMEM((requests, width), BF16),
        in_specs=[anywhere, local] + [anywhere] * 9,
        out_specs=local,
        scratch_shapes=[
            pltpu.SMEM(token_ids.shape, jnp.int32),
            pltpu.VMEM(retained.shape, BF16),
            pltpu.VMEM(query_weight.shape, BF16),
            pltpu.VMEM(key_weight.shape, BF16),
            pltpu.VMEM(value_weight.shape, BF16),
            pltpu.VMEM(gate_rows.shape, BF16),
            pltpu.VMEM(gate_bias.shape, F32),
            pltpu.VMEM(norm_gain.shape, F32),
            pltpu.VMEM(read_gain.shape, F32),
            pltpu.VMEM(out_weight.shape, BF16),
            pltpu.VMEM((parts, head_count, n, width), BF16),
            pltpu.VMEM((layers, parts, feat_count, n, span + LANES), BF16),
            pltpu.VMEM((layers, parts, max(heads - 1, 1), feat_count, n, span), BF16),
            pltpu.VMEM((layers, parts, heads, feat_count, n, 2 * head_size), BF16),
            pltpu.VMEM((layers, parts, heads, feat_count, n * group, head_size), BF16),
            pltpu.VMEM((layers, parts, chunks, head_count, n, width // chunks), BF16),
            pltpu.VMEM((pl.cdiv(block, LANES), n, LANES), jnp.int32),
            pltpu.VMEM((pl.cdiv(block, LANES), n, LANES), jnp.int32),
            pltpu.VMEM((pl.cdiv(block, LANES), n, LANES), F32),
            pltpu.VMEM((2, pl.cdiv(block, LANES), 8 * n, LANES), F32),
            pltpu.VMEM((8 * n, head_size), F32),
            pltpu.SemaphoreType.DMA((layers, 9)),
            pltpu.SemaphoreType.DMA((layers, requests)),
            pltpu.SemaphoreType.DMA((copies,)),
            pltpu.SemaphoreType.DMA((copies,)),
            pltpu.SemaphoreType.REGULAR((2,)),
        ],
        compiler_params=pltpu.CompilerParams(
            collective_id=0, has_side_effects=True, vmem_limit_bytes=66_000_000
        ),
    )(
        token_ids,
        pltpu.with_memory_space_constraint(picked, pltpu.VMEM),
        retained,
        query_weight,
        key_weight,
        value_weight,
        gate_rows,
        gate_bias,
        norm_gain,
        read_gain,
        out_weight,
    )


def solution(mesh):
    return jax.shard_map(
        functools.partial(body, mesh.shape["feat"], mesh.shape["head"]),
        mesh=mesh,
        in_specs=(
            P("groups"),
            P("head", "feat"),
            P(None, "groups", "head", "feat", None),
            P(None, "feat", "head"),
            P(None, "feat", "head"),
            P(None, "feat", "head"),
            P(None, "feat", "head"),
            P(None, "head"),
            P(None, "feat"),
            P(),
            P(None, "head", "feat"),
        ),
        out_specs=P("groups", "feat"),
        check_vma=False,
    )
```
